32 devices in a mesh: row: 4 (over y, x), col: 8 (over z, core).
Axes of the slice: x: 2, y: 2, z: 4, core: 2. Of those that a mesh axis runs over, the one named last changes fastest.
Arguments:
- tokens: bfloat16 [512, 8192], P('row', 'col'), may hold values from -6 to 6
- cotangent: bfloat16 [512, 8192], P('row', 'col'), may hold values from -0.25 to 0.25
- up_blocks: bfloat16 [128, 16, 128, 128], P('col', 'row'), may hold values from -0.125 to 0.125
- up_cols: int32 [128, 16], P('col', 'row'), may hold values from 0 to 63, as said below
- down_blocks: bfloat16 [128, 16, 128, 128], P('col', 'row'), may hold values from -0.125 to 0.125
- down_cols: int32 [128, 16], P('col', 'row'), may hold values from 0 to 63, as said below
Outputs:
- hidden: bfloat16 [512, 16384], P('row', 'col')
- grad_up: bfloat16 [128, 16, 128, 128], P('col', 'row')
- grad_down: bfloat16 [128, 16, 128, 128], P('col', 'row')
The draws below stay inside these ranges and needn't reach their ends.
Inputs may be any that keep to these rules, and one draw needn't show every extreme that they name: `up_cols`: each block row names 16 different block columns. `down_cols`: each block row names 16 different block columns.
All inputs are finite; a program needn't handle non-finite values.
Results may differ from the reference program's by a relative error of at most 0.014.
Values may be sent and summed in bfloat16 or wider, within the bound.
A program may use at most 128 MiB of HBM per device.

```python
import jax
import jax.numpy as jnp
from jax import lax

D = 8192
FF = 16384
BLK = 128
TOK_DEV = 128
TOKENS = 512
NBR = 128
K = 16
N_ROW = 4


def column_table(key):
    keys = jax.random.split(key, FF // BLK)
    perms = jax.vmap(lambda one: jax.random.permutation(one, D // BLK))(keys)
    return perms[:, :D // BLK // 4].astype(jnp.int32)


def draw_up_cols(key, part):
    return column_table(jax.random.fold_in(key, 11))


def draw_down_cols(key, part):
    return column_table(jax.random.fold_in(key, 23))


def levels(own_key, dims, pieces, low, top_value):
    def one(position, blocks):
        steps = jax.random.uniform(jax.random.fold_in(jax.random.fold_in(own_key, 6), position), (blocks,), jnp.float32, low / len(pieces), top_value / len(pieces))
        return jnp.repeat(jnp.exp(steps), dims[position] // blocks).reshape((-1,) + (1,) * (len(dims) - position - 1))

    gain = one(*pieces[0])
    for cut in pieces[1:]:
        gain = gain * one(*cut)
    return gain


def centred(own_key, shape, spread, most, cuts=(), kind=jnp.bfloat16):
    entries = spread * jax.random.normal(own_key, shape, jnp.float32)
    if cuts:
        entries = entries * levels(own_key, shape, cuts, -0.22, 0.18)
    return jnp.clip(entries, -most, most).astype(kind)


def setup_inputs(seed: int = 0) -> dict:
    key_list = jax.random.split(jax.random.key(seed), 7)
    return {
        "tokens": centred(key_list[0], (TOKENS, D), 1.0, 6.0, ((0, 4), (1, 8))),
        "cotangent": centred(key_list[1], (TOKENS, D), TOKENS ** -0.5, 0.25, ((0, 4), (1, 8))),
        "up_blocks": centred(key_list[2], (NBR, K, BLK, BLK), (K * BLK) ** -0.5, 0.125, ((0, 8), (1, 4))),
        "up_cols": draw_up_cols(jax.random.fold_in(key_list[6], 71), 0),
        "down_blocks": centred(key_list[4], (NBR, K, BLK, BLK), (K * BLK) ** -0.5, 0.125, ((0, 8), (1, 4))),
        "down_cols": draw_down_cols(jax.random.fold_in(key_list[6], 71), 0),
    }


def pick_blocks(rows, cols):
    shaped = rows.reshape(rows.shape[0], D // BLK, BLK)
    return jnp.take(shaped, cols, axis=1).astype(jnp.float32)


def reference(tokens, cotangent, up_blocks, up_cols, down_blocks, down_cols):
    w_up = up_blocks.astype(jnp.float32)
    w_down = down_blocks.astype(jnp.float32)

    def group(carry, index):
        start = (index * TOK_DEV).astype(jnp.int32)
        rows = lax.dynamic_slice_in_dim(tokens, start, TOK_DEV, 0)
        backs = lax.dynamic_slice_in_dim(cotangent, start, TOK_DEV, 0)
        in_sel = pick_blocks(rows, up_cols)
        pre = jnp.einsum("tikd,ikdf->tif", in_sel, w_up)
        act = jax.nn.silu(pre).astype(jnp.bfloat16)
        back_sel = pick_blocks(backs, down_cols)
        back = jnp.einsum("tikd,ikfd->tif", back_sel, w_down)
        sig = jax.nn.sigmoid(pre)
        slope = (back * sig * (1.0 + pre * (1.0 - sig))).astype(jnp.bfloat16)
        part_up = jnp.einsum("tikd,tif->ikdf", in_sel, slope.astype(jnp.float32)).astype(jnp.bfloat16)
        part_down = jnp.einsum("tif,tikd->ikfd", act.astype(jnp.float32), back_sel).astype(jnp.bfloat16)
        part_up, part_down = lax.optimization_barrier((part_up, part_down))
        total_up = carry[0] + part_up.astype(jnp.float32)
        total_down = carry[1] + part_down.astype(jnp.float32)
        return (total_up, total_down), act.reshape(TOK_DEV, FF)

    init = (jnp.zeros((NBR, K, BLK, BLK), jnp.float32), jnp.zeros((NBR, K, BLK, BLK), jnp.float32))
    totals, acts = lax.scan(group, init, jnp.arange(N_ROW, dtype=jnp.int32))
    hidden = acts.reshape(TOKENS, FF)
    return (hidden, totals[0].astype(jnp.bfloat16), totals[1].astype(jnp.bfloat16))
```

```python
import functools

import jax
import jax.numpy as jnp
from jax import lax
from jax.experimental import pallas as pl
from jax.experimental.pallas import tpu as pltpu
from jax.sharding import PartitionSpec as P

MESH = pl.DeviceIdType.MESH
ANY = pl.BlockSpec(memory_space=pl.ANY)
VM = pl.BlockSpec(memory_space=pltpu.VMEM)
f32 = jnp.float32
bf16 = jnp.bfloat16


def place():
    r = lax.axis_index("row")
    c = lax.axis_index("col")
    xn = r + 1 - 2 * (r % 2)
    yn = (r + 2) % 4
    return r, c, xn, yn, 3 - r


class Puts:
    def __init__(self, sems):
        self.sems = sems
        self.copies = []

    def __call__(self, src, dst, recv, dev):
        cp = pltpu.make_async_remote_copy(
            src_ref=src, dst_ref=dst, send_sem=self.sems.at[len(self.copies)],
            recv_sem=recv, device_id=dev, device_id_type=MESH)
        cp.start()
        self.copies.append(cp)

    def got(self, ref, recv, dev):
        pltpu.make_async_remote_copy(
            src_ref=ref, dst_ref=ref, send_sem=self.sems.at[0],
            recv_sem=recv, device_id=dev, device_id_type=MESH).wait_recv()

    def drain(self):
        for cp in self.copies:
            cp.wait_send()


def greet(devs):
    sem = pltpu.get_barrier_semaphore()
    for dev in devs:
        pl.semaphore_signal(sem, inc=1, device_id=dev, device_id_type=MESH)
    pl.semaphore_wait(sem, len(devs))


def gather_kernel(tok, cot, wu, wd, ci, T, G, WU, WD, CI, own, send, recv, wrecv, loc):
    r, c, xn, yn, dg = place()
    z, q = c // 2, c % 2
    pc = c + 1 - 2 * q
    zcs = [((z + d) % 4) * 2 + q for d in range(4)]
    zps = [((z + d) % 4) * 2 + 1 - q for d in range(4)]
    X, Y, D, Q = (xn, c), (yn, c), (dg, c), (r, pc)
    greet([(r, zc) for zc in zcs[1:]] + [X, Y, D, Q])
    put = Puts(send)

    def fwd(a, rr, cc, dev, src=None):
        ref = (T, G)[a].at[rr, cc]
        put(ref if src is None else src, ref, recv.at[a, rr, cc], dev)

    def got(a, rr, cc):
        put.got((T, G)[a].at[rr, cc], recv.at[a, rr, cc], Q)

    ins = [pltpu.make_async_copy(w.at[r], own.at[j], loc.at[j]) for j, w in enumerate((wu, wd))]
    for cp in ins:
        cp.start()
    outs = [
        pltpu.make_async_copy(tok, T.at[r, c], loc.at[2]),
        pltpu.make_async_copy(cot, G.at[r, c], loc.at[3]),
        pltpu.make_async_copy(ci.at[r], CI.at[r], loc.at[4]),
    ]
    for cp in outs:
        cp.start()
    for d in (1, 3, 2):
        for a, s in enumerate((tok, cot)):
            fwd(a, r, c, (r, zcs[d]), s)
    fwd(0, r, c, X, tok)
    fwd(1, r, c, Y, cot)
    fwd(1, r, c, X, cot)
    fwd(0, r, c, Y, tok)
    fwd(0, r, c, Q, tok)
    fwd(1, r, c, Q, cot)
    for peer in (dg, xn, yn):
        for j, (s, t) in enumerate(((wu, WU), (wd, WD), (ci, CI))):
            put(s.at[peer], t.at[r], wrecv.at[j, r], (peer, c))
    for j, cp in enumerate(ins):
        cp.wait()
        cp = pltpu.make_async_copy(own.at[j], (WU, WD)[j].at[r], loc.at[5 + j])
        cp.start()
        outs.append(cp)

    def relay(cc):
        got(0, xn, cc)
        fwd(0, xn, cc, Y)
        fwd(0, xn, cc, Q)
        got(1, yn, cc)
        fwd(1, yn, cc, X)
        fwd(1, yn, cc, Q)

    order = (0, 1, 3, 2)
    for n, d in enumerate(order):
        if n:
            got(0, r, zcs[d])
            fwd(0, r, zcs[d], X)
            got(1, r, zcs[d])
            fwd(1, r, zcs[d], Y)
            fwd(1, r, zcs[d], X)
            fwd(0, r, zcs[d], Y)
            fwd(0, r, zcs[d], Q)
            fwd(1, r, zcs[d], Q)
            relay(zcs[order[n - 1]])
    relay(zcs[order[3]])
    for d in order:
        for a, rr in ((1, xn), (0, yn), (0, dg), (1, dg)):
            got(a, rr, zcs[d])
            fwd(a, rr, zcs[d], Q)
    for peer in (dg, xn, yn):
        for j, t in enumerate((WU, WD, CI)):
            put.got(t.at[peer], wrecv.at[j, peer], (peer, c))
    for d in order:
        for rr in (r, xn, yn, dg):
            for a in range(2):
                got(a, rr, zps[d])
    for cp in outs:
        cp.wait()
    put.drain()


def gather_all(tok, cot, wu, wd, ci):
    full = jax.ShapeDtypeStruct((4, 8) + tok.shape, bf16)
    return pl.pallas_call(
        gather_kernel,
        out_shape=(full, full, jax.ShapeDtypeStruct(wu.shape, bf16),
                   jax.ShapeDtypeStruct(wd.shape, bf16), jax.ShapeDtypeStruct(ci.shape, ci.dtype)),
        in_specs=[VM, VM, ANY, ANY, ANY],
        out_specs=(ANY,) * 5,
        scratch_shapes=[
            pltpu.VMEM((2,) + wu.shape[1:], bf16),
            pltpu.SemaphoreType.DMA((80,)),
            pltpu.SemaphoreType.DMA((2, 4, 8)),
            pltpu.SemaphoreType.DMA((3, 4)),
            pltpu.SemaphoreType.DMA((7,)),
        ],
        compiler_params=pltpu.CompilerParams(collective_id=0, has_side_effects=True),
        name="gather_all",
    )(tok, cot, wu, wd, ci)


def row_kernel(ci, T, G, wu, wd, hid, gu, gd, xs, gs, ws):
    i = pl.program_id(0)
    for k in range(16):
        for a, (src, dst) in enumerate(((T, xs), (G, gs))):
            b = ci[k // 4, 0, a * 16 + i * 4 + k % 4]
            lo = pl.multiple_of((b % 8) * 128, 128)
            dst[:, k * 128:(k + 1) * 128] = src[:, b // 8, :, pl.ds(lo, 128)].reshape(512, 128)
        ws[:, k * 128:(k + 1) * 128] = wd[k // 4, 0, k % 4]
    pre = jnp.dot(xs[...], wu[...].reshape(2048, 128), preferred_element_type=f32)
    back = lax.dot_general(gs[...], ws[...], (((1,), (1,)), ((), ())), preferred_element_type=f32)
    sig = jax.nn.sigmoid(pre)
    act = (pre * sig).astype(bf16)
    slope = (back * sig * (1.0 + pre * (1.0 - sig))).astype(bf16)
    hid[...] = act.reshape(4, 128, 128)
    act_t = act.T
    slope_t = slope.T
    for k in range(0, 16, 4):
        cols = slice(k * 128, (k + 4) * 128)
        down = jnp.dot(act_t, gs[:, cols], preferred_element_type=f32)
        up = jnp.dot(slope_t, xs[:, cols], preferred_element_type=f32)
        for j in range(4):
            gd[k // 4, 0, j] = down[:, j * 128:(j + 1) * 128].astype(bf16)
            gu[k // 4, 0, j] = up[:, j * 128:(j + 1) * 128].T.astype(bf16)


def rows_all(ci, T, G, wu, wd):
    whole = pl.BlockSpec(T.shape, lambda i, s: (0, 0, 0, 0), pipeline_mode=pl.Buffered(1))
    wspec = pl.BlockSpec((4, 1, 4, 128, 128), lambda i, s: (0, i, 0, 0, 0))
    return pl.pallas_call(
        row_kernel,
        out_shape=(jax.ShapeDtypeStruct((4, 128, 512), bf16),
                   jax.ShapeDtypeStruct(wu.shape, bf16), jax.ShapeDtypeStruct(wd.shape, bf16)),
        grid_spec=pltpu.PrefetchScalarGridSpec(
            num_scalar_prefetch=1, grid=(4,),
            in_specs=[whole, whole, wspec, wspec],
            out_specs=(pl.BlockSpec((4, 128, 128), lambda i, s: (0, 0, i)), wspec, wspec),
            scratch_shapes=[pltpu.VMEM((512, 2048), bf16), pltpu.VMEM((512, 2048), bf16),
                            pltpu.VMEM((128, 2048), bf16)]),
        compiler_params=pltpu.CompilerParams(vmem_limit_bytes=48 << 20),
        name="rows_all",
    )(ci, T, G, wu, wd)


def scatter_kernel(hid, gu, gd, H, U, Dn, vh, vw, send, recv, loc):
    r, c, xn, yn, dg = place()
    peers = (dg, xn, yn)
    greet([(p, c) for p in peers])
    put = Puts(send)

    def dests(rr):
        return (H.at[:, pl.ds(pl.multiple_of(rr * 512, 512), 512)],
                U.at[pl.ds(rr * 4, 4)], Dn.at[pl.ds(rr * 4, 4)])

    mine = dests(r)
    ins = [pltpu.make_async_copy(s.at[r], v, loc.at[j])
           for j, (s, v) in enumerate(((hid, vh), (gu, vw.at[0]), (gd, vw.at[1])))]
    for cp in ins:
        cp.start()
    for p in peers:
        for j, s in enumerate((hid, gu, gd)):
            put(s.at[p], mine[j], recv.at[j, r], (p, c))
    outs = []
    for j, v in enumerate((vh, vw.at[0], vw.at[1])):
        ins[j].wait()
        cp = pltpu.make_async_copy(v, mine[j], loc.at[3 + j])
        cp.start()
        outs.append(cp)
    for p in peers:
        for j, t in enumerate(dests(p)):
            put.got(t, recv.at[j, p], (p, c))
    for cp in outs:
        cp.wait()
    put.drain()


def scatter_all(hid, gu, gd):
    grad = jax.ShapeDtypeStruct((16,) + gu.shape[2:], bf16)
    return pl.pallas_call(
        scatter_kernel,
        out_shape=(jax.ShapeDtypeStruct((128, 2048), bf16), grad, grad),
        in_specs=[ANY, ANY, ANY],
        out_specs=(ANY,) * 3,
        scratch_shapes=[
            pltpu.VMEM(hid.shape[1:], bf16),
            pltpu.VMEM((2,) + gu.shape[1:], bf16),
            pltpu.SemaphoreType.DMA((9,)),
            pltpu.SemaphoreType.DMA((3, 4)),
            pltpu.SemaphoreType.DMA((6,)),
        ],
        compiler_params=pltpu.CompilerParams(collective_id=1, has_side_effects=True),
        name="scatter_all",
    )(hid, gu, gd)


def per_row(tokens, cotangent, up_blocks, up_cols, down_blocks, down_cols):
    wu = up_blocks.reshape(4, 4, 4, 128, 128)
    wd = down_blocks.reshape(4, 4, 4, 128, 128)
    ci = jnp.concatenate([up_cols.reshape(4, 16), down_cols.reshape(4, 16)], axis=1)
    ci = jnp.pad(ci[:, None, :], ((0, 0), (0, 7), (0, 96)))
    T, G, WU, WD, CI = gather_all(tokens, cotangent, wu, wd, ci)
    hid, gu, gd = rows_all(CI, T, G, WU, WD)
    return scatter_all(hid, gu, gd)


def per_device(tokens, cotangent, up_blocks, up_cols, down_blocks, down_cols):
    rows = tokens.shape[0]
    local_rows = up_blocks.shape[0]
    side = up_blocks.shape[2]
    whole_up, up_index, whole_down, down_index = (
        lax.all_gather(up_blocks, "row", axis=1, tiled=True),
        lax.all_gather(up_cols, "row", axis=1, tiled=True),
        lax.all_gather(down_blocks, "row", axis=1, tiled=True),
        lax.all_gather(down_cols, "row", axis=1, tiled=True),
    )
    piece_in = lax.all_gather(tokens, "col", axis=1, tiled=True)
    piece_back = lax.all_gather(cotangent, "col", axis=1, tiled=True)
    width = piece_in.shape[1] // side
    in_piece = piece_in.reshape(rows, width, side)
    back_piece = piece_back.reshape(rows, width, side)
    idents = jnp.arange(width, dtype=jnp.int32)
    pick_up = (up_index[:, :, None] == idents[None, None, :]).astype(jnp.bfloat16)
    pick_down = (down_index[:, :, None] == idents[None, None, :]).astype(jnp.bfloat16)
    in_sel = jnp.einsum(
        "tcd,ikc->tikd", in_piece, pick_up, preferred_element_type=jnp.float32
    ).astype(jnp.bfloat16)
    back_sel = jnp.einsum(
        "tcd,ikc->tikd", back_piece, pick_down, preferred_element_type=jnp.float32
    ).astype(jnp.bfloat16)
    in_sel, back_sel = (in_sel, back_sel)
    pre = jnp.einsum("tikd,ikdf->tif", in_sel, whole_up, preferred_element_type=jnp.float32)
    back = jnp.einsum("tikd,ikfd->tif", back_sel, whole_down, preferred_element_type=jnp.float32)
    act = jax.nn.silu(pre).astype(jnp.bfloat16)
    part_down = jnp.einsum("tif,tikd->ikfd", act, back_sel, preferred_element_type=jnp.float32)
    sig = jax.nn.sigmoid(pre)
    slope = (back * sig * (1.0 + pre * (1.0 - sig))).astype(jnp.bfloat16)
    part_up = jnp.einsum("tikd,tif->ikdf", in_sel, slope, preferred_element_type=jnp.float32)
    grad_up, grad_down = (
        lax.psum_scatter(
            part_up.astype(jnp.bfloat16).astype(jnp.float32).astype(jnp.bfloat16),
            "row",
            scatter_dimension=1,
            tiled=True,
        ).astype(jnp.float32),
        lax.psum_scatter(
            part_down.astype(jnp.bfloat16).astype(jnp.float32).astype(jnp.bfloat16),
            "row",
            scatter_dimension=1,
            tiled=True,
        ).astype(jnp.float32),
    )
    hidden = act.reshape(rows, local_rows * side)
    return (hidden, grad_up.astype(jnp.bfloat16), grad_down.astype(jnp.bfloat16))


def solution(mesh):
    small = mesh.shape["row"] == 4 and mesh.shape["col"] == 8
    return jax.shard_map(
        per_row if small else per_device,
        mesh=mesh,
        in_specs=(
            P("row", "col"),
            P("row", "col"),
            P("col", "row", None, None),
            P("col", "row"),
            P("col", "row", None, None),
            P("col", "row"),
        ),
        out_specs=(P("row", "col"), P("col", "row", None, None), P("col", "row", None, None)),
        check_vma=False,
    )
```

```python
import functools

import jax
import jax.numpy as jnp
from jax import lax
from jax.experimental import pallas as pl
from jax.experimental.pallas import tpu as pltpu
from jax.sharding import PartitionSpec as P

MESH = pl.DeviceIdType.MESH
ANY = pl.BlockSpec(memory_space=pl.ANY)
VM = pl.BlockSpec(memory_space=pltpu.VMEM)
f32 = jnp.float32
bf16 = jnp.bfloat16


def place():
    r = lax.axis_index("row")
    c = lax.axis_index("col")
    xn = r + 1 - 2 * (r % 2)
    yn = (r + 2) % 4
    return r, c, xn, yn, 3 - r


class Puts:
    def __init__(self, sems):
        self.sems = sems
        self.copies = []

    def __call__(self, src, dst, recv, dev, when=None):
        cp = pltpu.make_async_remote_copy(
            src_ref=src, dst_ref=dst, send_sem=self.sems.at[len(self.copies)],
            recv_sem=recv, device_id=dev, device_id_type=MESH)
        if when is None:
            cp.start()
        else:
            pl.when(when)(cp.start)
        self.copies.append((cp, when))

    def got(self, ref, recv, dev):
        pltpu.make_async_remote_copy(
            src_ref=ref, dst_ref=ref, send_sem=self.sems.at[0],
            recv_sem=recv, device_id=dev, device_id_type=MESH).wait_recv()

    def drain(self):
        for cp, when in self.copies:
            if when is None:
                cp.wait_send()
            else:
                pl.when(when)(cp.wait_send)


def greet(devs):
    sem = pltpu.get_barrier_semaphore()
    for dev in devs:
        pl.semaphore_signal(sem, inc=1, device_id=dev, device_id_type=MESH)
    pl.semaphore_wait(sem, len(devs))


def gather_kernel(tok, cot, wu, wd, ci, T, G, WU, WD, CI, own, send, recv, wrecv, loc):
    r, c, xn, yn, dg = place()
    z, q = c // 2, c % 2
    pc = c + 1 - 2 * q
    first = xn + q * (yn - xn)
    second = yn + q * (xn - yn)
    zcs = [((z + d) % 4) * 2 + q for d in range(4)]
    X, Y, D, Q = (xn, c), (yn, c), (dg, c), (r, pc)
    rows = (r, xn, yn, dg)
    greet([(r, zc) for zc in zcs[1:]] + [X, Y, D, Q])
    put = Puts(send)

    def fwd(a, rr, cc, dev, src=None, when=None):
        ref = (T, G)[a].at[rr, cc]
        put(ref if src is None else src, ref, recv.at[a, rr, cc], dev, when)

    def got(a, rr, cc):
        put.got((T, G)[a].at[rr, cc], recv.at[a, rr, cc], Q)

    ins = [pltpu.make_async_copy(w.at[r], own.at[j], loc.at[j]) for j, w in enumerate((wu, wd))]
    for cp in ins:
        cp.start()
    outs = [
        pltpu.make_async_copy(tok, T.at[r, c], loc.at[2]),
        pltpu.make_async_copy(cot, G.at[r, c], loc.at[3]),
        pltpu.make_async_copy(ci, CI.at[r], loc.at[4]),
    ]
    for cp in outs:
        cp.start()

    def along(rr, src=None):
        fwd(1, rr, c, (r, c + 2), src, z < 3)
        fwd(1, rr, c, (r, c - 2), src, z > 0)

    def weights(j):
        for peer in (dg, xn, yn):
            put((wu, wd)[j].at[peer], (WU, WD)[j].at[r], wrecv.at[j, r], (peer, c))

    fwd(1, r, c, X, cot)
    fwd(1, r, c, Y, cot)
    for d in (1, 3, 2):
        fwd(0, r, c, (r, zcs[d]), tok)
    fwd(0, r, c, X, tok)
    fwd(0, r, c, Y, tok)
    along(r, cot)
    fwd(0, r, c, Q, tok)
    fwd(1, r, c, Q, cot)
    for peer in (dg, xn, yn):
        put(ci, CI.at[r], wrecv.at[2, r], (peer, c))
    got(1, first, c)
    fwd(1, first, c, (second, c))
    got(1, second, c)
    for rr in (first, second):
        along(rr)
        fwd(1, rr, c, Q)
    weights(0)
    got(1, dg, c)
    along(dg)
    fwd(1, dg, c, Q)
    for j, cp in enumerate(ins):
        cp.wait()
        cp = pltpu.make_async_copy(own.at[j], (WU, WD)[j].at[r], loc.at[5 + j])
        cp.start()
        outs.append(cp)

    def relay(d):
        got(0, first, zcs[d])
        fwd(0, first, zcs[d], (second, c))
        fwd(0, first, zcs[d], Q)

    def onward(step):
        for sign in (1, -1):
            here = z >= step if sign == 1 else z + step < 4
            more = z < 3 if sign == 1 else z > 0
            cc = c - 2 * sign * step
            for rr in rows:
                pl.when(here)(functools.partial(got, 1, rr, cc))
                if step < 3:
                    fwd(1, rr, cc, (r, c + 2 * sign), None, here & more)
                fwd(1, rr, cc, Q, None, here)

    for d in (1, 3, 2):
        got(0, r, zcs[d])
        fwd(0, r, zcs[d], X)
        fwd(0, r, zcs[d], Y)
        fwd(0, r, zcs[d], Q)
    relay(0)
    relay(1)
    onward(1)
    relay(3)
    relay(2)
    weights(1)
    for d in (0, 1):
        for rr in (second, dg):
            got(0, rr, zcs[d])
            fwd(0, rr, zcs[d], Q)
    onward(2)
    for d in (3, 2):
        for rr in (second, dg):
            got(0, rr, zcs[d])
            fwd(0, rr, zcs[d], Q)
    onward(3)
    for j, t in enumerate((WU, WD, CI)):
        for peer in (dg, xn, yn):
            put.got(t.at[peer], wrecv.at[j, peer], (peer, c))
    for a in range(2):
        for d in range(4):
            for rr in rows:
                got(a, rr, ((z + d) % 4) * 2 + 1 - q)
    for cp in outs:
        cp.wait()
    put.drain()


def gather_all(tok, cot, wu, wd, ci):
    full = jax.ShapeDtypeStruct((4, 8) + tok.shape, bf16)
    return pl.pallas_call(
        gather_kernel,
        out_shape=(full, full, jax.ShapeDtypeStruct(wu.shape, bf16),
                   jax.ShapeDtypeStruct(wd.shape, bf16), jax.ShapeDtypeStruct((4,) + ci.shape, ci.dtype)),
        in_specs=[VM, VM, ANY, ANY, ANY],
        out_specs=(ANY,) * 5,
        scratch_shapes=[
            pltpu.VMEM((2,) + wu.shape[1:], bf16),
            pltpu.SemaphoreType.DMA((96,)),
            pltpu.SemaphoreType.DMA((2, 4, 8)),
            pltpu.SemaphoreType.DMA((3, 4)),
            pltpu.SemaphoreType.DMA((7,)),
        ],
        compiler_params=pltpu.CompilerParams(collective_id=0, has_side_effects=True),
        name="gather_all",
    )(tok, cot, wu, wd, ci)


def row_kernel(ci, T, G, wu, wd, hid, gu, gd, xs, gs, ws):
    i = pl.program_id(0)
    row = lax.axis_index("row") * 4 + i
    for k in range(16):
        for a, (src, dst) in enumerate(((T, xs), (G, gs))):
            b = ci[k // 4, a * 4 + k % 4, row]
            lo = pl.multiple_of((b % 8) * 128, 128)
            dst[:, k * 128:(k + 1) * 128] = src[:, b // 8, :, pl.ds(lo, 128)].reshape(512, 128)
        ws[:, k * 128:(k + 1) * 128] = wd[k // 4, 0, k % 4]
    pre = jnp.dot(xs[...], wu[...].reshape(2048, 128), preferred_element_type=f32)
    back = lax.dot_general(gs[...], ws[...], (((1,), (1,)), ((), ())), preferred_element_type=f32)
    sig = jax.nn.sigmoid(pre)
    act = (pre * sig).astype(bf16)
    slope = (back * sig * (1.0 + pre * (1.0 - sig))).astype(bf16)
    hid[...] = act.reshape(4, 128, 128)
    act_t = act.T
    slope_t = slope.T
    for k in range(0, 16, 4):
        cols = slice(k * 128, (k + 4) * 128)
        down = jnp.dot(act_t, gs[:, cols], preferred_element_type=f32)
        up = jnp.dot(slope_t, xs[:, cols], preferred_element_type=f32)
        for j in range(4):
            gd[k // 4, 0, j] = down[:, j * 128:(j + 1) * 128].astype(bf16)
            gu[k // 4, 0, j] = up[:, j * 128:(j + 1) * 128].T.astype(bf16)


def rows_all(ci, T, G, wu, wd):
    whole = pl.BlockSpec(T.shape, lambda i, s: (0, 0, 0, 0), pipeline_mode=pl.Buffered(1))
    wspec = pl.BlockSpec((4, 1, 4, 128, 128), lambda i, s: (0, i, 0, 0, 0))
    return pl.pallas_call(
        row_kernel,
        out_shape=(jax.ShapeDtypeStruct((4, 128, 512), bf16),
                   jax.ShapeDtypeStruct(wu.shape, bf16), jax.ShapeDtypeStruct(wd.shape, bf16)),
        grid_spec=pltpu.PrefetchScalarGridSpec(
            num_scalar_prefetch=1, grid=(4,),
            in_specs=[whole, whole, wspec, wspec],
            out_specs=(pl.BlockSpec((4, 128, 128), lambda i, s: (0, 0, i)), wspec, wspec),
            scratch_shapes=[pltpu.VMEM((512, 2048), bf16), pltpu.VMEM((512, 2048), bf16),
                            pltpu.VMEM((128, 2048), bf16)]),
        compiler_params=pltpu.CompilerParams(vmem_limit_bytes=48 << 20),
        name="rows_all",
    )(ci, T, G, wu, wd)


def scatter_kernel(hid, gu, gd, H, U, Dn, send, recv, loc):
    r, c, xn, yn, dg = place()
    peers = (dg, xn, yn)
    greet([(p, c) for p in peers])
    put = Puts(send)

    def dests(rr):
        return (U.at[pl.ds(rr * 4, 4)], Dn.at[pl.ds(rr * 4, 4)],
                H.at[:, pl.ds(pl.multiple_of(rr * 512, 512), 512)])

    mine = dests(r)
    for p in peers:
        for j, s in enumerate((gu, gd, hid)):
            put(s.at[p], mine[j], recv.at[j, r], (p, c))
    outs = [pltpu.make_async_copy(s.at[r], mine[j], loc.at[j]) for j, s in enumerate((gu, gd, hid))]
    for cp in outs:
        cp.start()
    for p in peers:
        for j, t in enumerate(dests(p)):
            put.got(t, recv.at[j, p], (p, c))
    for cp in outs:
        cp.wait()
    put.drain()


def scatter_all(hid, gu, gd):
    grad = jax.ShapeDtypeStruct((16,) + gu.shape[2:], bf16)
    return pl.pallas_call(
        scatter_kernel,
        out_shape=(jax.ShapeDtypeStruct((128, 2048), bf16), grad, grad),
        in_specs=[VM] * 3,
        out_specs=(ANY,) * 3,
        scratch_shapes=[
            pltpu.SemaphoreType.DMA((9,)),
            pltpu.SemaphoreType.DMA((3, 4)),
            pltpu.SemaphoreType.DMA((3,)),
        ],
        compiler_params=pltpu.CompilerParams(collective_id=1, has_side_effects=True),
        name="scatter_all",
    )(hid, gu, gd)


def per_row(tokens, cotangent, up_blocks, up_cols, down_blocks, down_cols):
    wu = up_blocks.reshape(4, 4, 4, 128, 128)
    wd = down_blocks.reshape(4, 4, 4, 128, 128)
    ci = jnp.concatenate([up_cols.T, down_cols.T], axis=0)
    ci = jnp.pad(ci, ((0, 0), (0, 112)))
    T, G, WU, WD, CI = gather_all(tokens, cotangent, wu, wd, ci)
    hid, gu, gd = rows_all(CI, T, G, WU, WD)
    return scatter_all(hid, gu, gd)


def per_device(tokens, cotangent, up_blocks, up_cols, down_blocks, down_cols):
    rows = tokens.shape[0]
    local_rows = up_blocks.shape[0]
    side = up_blocks.shape[2]
    whole_up, up_index, whole_down, down_index = (
        lax.all_gather(up_blocks, "row", axis=1, tiled=True),
        lax.all_gather(up_cols, "row", axis=1, tiled=True),
        lax.all_gather(down_blocks, "row", axis=1, tiled=True),
        lax.all_gather(down_cols, "row", axis=1, tiled=True),
    )
    piece_in = lax.all_gather(tokens, "col", axis=1, tiled=True)
    piece_back = lax.all_gather(cotangent, "col", axis=1, tiled=True)
    width = piece_in.shape[1] // side
    in_piece = piece_in.reshape(rows, width, side)
    back_piece = piece_back.reshape(rows, width, side)
    idents = jnp.arange(width, dtype=jnp.int32)
    pick_up = (up_index[:, :, None] == idents[None, None, :]).astype(jnp.bfloat16)
    pick_down = (down_index[:, :, None] == idents[None, None, :]).astype(jnp.bfloat16)
    in_sel = jnp.einsum(
        "tcd,ikc->tikd", in_piece, pick_up, preferred_element_type=jnp.float32
    ).astype(jnp.bfloat16)
    back_sel = jnp.einsum(
        "tcd,ikc->tikd", back_piece, pick_down, preferred_element_type=jnp.float32
    ).astype(jnp.bfloat16)
    in_sel, back_sel = (in_sel, back_sel)
    pre = jnp.einsum("tikd,ikdf->tif", in_sel, whole_up, preferred_element_type=jnp.float32)
    back = jnp.einsum("tikd,ikfd->tif", back_sel, whole_down, preferred_element_type=jnp.float32)
    act = jax.nn.silu(pre).astype(jnp.bfloat16)
    part_down = jnp.einsum("tif,tikd->ikfd", act, back_sel, preferred_element_type=jnp.float32)
    sig = jax.nn.sigmoid(pre)
    slope = (back * sig * (1.0 + pre * (1.0 - sig))).astype(jnp.bfloat16)
    part_up = jnp.einsum("tikd,tif->ikdf", in_sel, slope, preferred_element_type=jnp.float32)
    grad_up, grad_down = (
        lax.psum_scatter(
            part_up.astype(jnp.bfloat16).astype(jnp.float32).astype(jnp.bfloat16),
            "row",
            scatter_dimension=1,
            tiled=True,
        ).astype(jnp.float32),
        lax.psum_scatter(
            part_down.astype(jnp.bfloat16).astype(jnp.float32).astype(jnp.bfloat16),
            "row",
            scatter_dimension=1,
            tiled=True,
        ).astype(jnp.float32),
    )
    hidden = act.reshape(rows, local_rows * side)
    return (hidden, grad_up.astype(jnp.bfloat16), grad_down.astype(jnp.bfloat16))


def solution(mesh):
    small = mesh.shape["row"] == 4 and mesh.shape["col"] == 8
    return jax.shard_map(
        per_row if small else per_device,
        mesh=mesh,
        in_specs=(
            P("row", "col"),
            P("row", "col"),
            P("col", "row", None, None),
            P("col", "row"),
            P("col", "row", None, None),
            P("col", "row"),
        ),
        out_specs=(P("row", "col"), P("col", "row", None, None), P("col", "row", None, None)),
        check_vma=False,
    )
```

```python
import functools

import jax
import jax.numpy as jnp
from jax import lax
from jax.experimental import pallas as pl
from jax.experimental.pallas import tpu as pltpu
from jax.sharding import PartitionSpec as P

MESH = pl.DeviceIdType.MESH
ANY = pl.BlockSpec(memory_space=pl.ANY)
VM = pl.BlockSpec(memory_space=pltpu.VMEM)
f32 = jnp.float32
bf16 = jnp.bfloat16


def place():
    r = lax.axis_index("row")
    c = lax.axis_index("col")
    xn = r + 1 - 2 * (r % 2)
    yn = (r + 2) % 4
    return r, c, xn, yn, 3 - r


class Puts:
    def __init__(self, sems):
        self.sems = sems
        self.copies = []

    def __call__(self, src, dst, recv, dev, when=None):
        cp = pltpu.make_async_remote_copy(
            src_ref=src, dst_ref=dst, send_sem=self.sems.at[len(self.copies)],
            recv_sem=recv, device_id=dev, device_id_type=MESH)
        if when is None:
            cp.start()
        else:
            pl.when(when)(cp.start)
        self.copies.append((cp, when))

    def got(self, ref, recv, dev):
        pltpu.make_async_remote_copy(
            src_ref=ref, dst_ref=ref, send_sem=self.sems.at[0],
            recv_sem=recv, device_id=dev, device_id_type=MESH).wait_recv()

    def drain(self):
        for cp, when in self.copies:
            if when is None:
                cp.wait_send()
            else:
                pl.when(when)(cp.wait_send)


def greet(devs):
    sem = pltpu.get_barrier_semaphore()
    for dev in devs:
        pl.semaphore_signal(sem, inc=1, device_id=dev, device_id_type=MESH)
    pl.semaphore_wait(sem, len(devs))


def gather_kernel(tok, cot, wu, wd, ci, T, G, WU, WD, CI, own, send, recv, wrecv, loc):
    r, c, xn, yn, dg = place()
    z, q = c // 2, c % 2
    pc = c + 1 - 2 * q
    first = xn + q * (yn - xn)
    second = yn + q * (xn - yn)
    zcs = [((z + d) % 4) * 2 + q for d in range(4)]
    X, Y, D, Q = (xn, c), (yn, c), (dg, c), (r, pc)
    rows = (r, xn, yn, dg)
    greet([(r, zc) for zc in zcs[1:]] + [X, Y, D, Q])
    put = Puts(send)

    def slot(a, rr, cc):
        return (T, G)[a].at[pl.ds(cc * 8, 8), rr]

    def fwd(a, rr, cc, dev, src=None, when=None):
        ref = slot(a, rr, cc)
        put(ref if src is None else src, ref, recv.at[a, rr, cc], dev, when)

    def got(a, rr, cc):
        put.got(slot(a, rr, cc), recv.at[a, rr, cc], Q)

    ins = [pltpu.make_async_copy(w.at[r], own.at[j], loc.at[j]) for j, w in enumerate((wu, wd))]
    for cp in ins:
        cp.start()
    outs = [
        pltpu.make_async_copy(tok, slot(0, r, c), loc.at[2]),
        pltpu.make_async_copy(cot, slot(1, r, c), loc.at[3]),
        pltpu.make_async_copy(ci, CI.at[r], loc.at[4]),
    ]
    for cp in outs:
        cp.start()

    def along(rr, src=None):
        fwd(1, rr, c, (r, c + 2), src, z < 3)
        fwd(1, rr, c, (r, c - 2), src, z > 0)

    def weights(j):
        for peer in (dg, xn, yn):
            put((wu, wd)[j].at[peer], (WU, WD)[j].at[r], wrecv.at[j, r], (peer, c))

    fwd(1, r, c, X, cot)
    fwd(1, r, c, Y, cot)
    for d in (1, 3, 2):
        fwd(0, r, c, (r, zcs[d]), tok)
    fwd(0, r, c, X, tok)
    fwd(0, r, c, Y, tok)
    along(r, cot)
    fwd(0, r, c, Q, tok)
    fwd(1, r, c, Q, cot)
    for peer in (dg, xn, yn):
        put(ci, CI.at[r], wrecv.at[2, r], (peer, c))
    got(1, first, c)
    fwd(1, first, c, (second, c))
    got(1, second, c)
    for rr in (first, second):
        along(rr)
        fwd(1, rr, c, Q)
    weights(0)
    got(1, dg, c)
    along(dg)
    fwd(1, dg, c, Q)
    for j, cp in enumerate(ins):
        cp.wait()
        cp = pltpu.make_async_copy(own.at[j], (WU, WD)[j].at[r], loc.at[5 + j])
        cp.start()
        outs.append(cp)

    def relay(d):
        got(0, first, zcs[d])
        fwd(0, first, zcs[d], (second, c))
        fwd(0, first, zcs[d], Q)

    def onward(step):
        for sign in (1, -1):
            here = z >= step if sign == 1 else z + step < 4
            more = z < 3 if sign == 1 else z > 0
            cc = c - 2 * sign * step
            for rr in rows:
                pl.when(here)(functools.partial(got, 1, rr, cc))
                if step < 3:
                    fwd(1, rr, cc, (r, c + 2 * sign), None, here & more)
                fwd(1, rr, cc, Q, None, here)

    for d in (1, 3, 2):
        got(0, r, zcs[d])
        fwd(0, r, zcs[d], X)
        fwd(0, r, zcs[d], Y)
        fwd(0, r, zcs[d], Q)
    relay(0)
    relay(1)
    onward(1)
    relay(3)
    relay(2)
    weights(1)
    for d in (0, 1):
        for rr in (second, dg):
            got(0, rr, zcs[d])
            fwd(0, rr, zcs[d], Q)
    onward(2)
    for d in (3, 2):
        for rr in (second, dg):
            got(0, rr, zcs[d])
            fwd(0, rr, zcs[d], Q)
    onward(3)
    for j, t in enumerate((WU, WD, CI)):
        for peer in (dg, xn, yn):
            put.got(t.at[peer], wrecv.at[j, peer], (peer, c))
    for a in range(2):
        for d in range(4):
            for rr in rows:
                got(a, rr, ((z + d) % 4) * 2 + 1 - q)
    for cp in outs:
        cp.wait()
    put.drain()


def gather_all(tok, cot, wu, wd, ci):
    full = jax.ShapeDtypeStruct((64, 4, 128, 128), bf16)
    return pl.pallas_call(
        gather_kernel,
        out_shape=(full, full, jax.ShapeDtypeStruct(wu.shape, bf16),
                   jax.ShapeDtypeStruct(wd.shape, bf16), jax.ShapeDtypeStruct((4,) + ci.shape, ci.dtype)),
        in_specs=[VM, VM, ANY, ANY, ANY],
        out_specs=(ANY,) * 5,
        scratch_shapes=[
            pltpu.VMEM((2,) + wu.shape[1:], bf16),
            pltpu.SemaphoreType.DMA((96,)),
            pltpu.SemaphoreType.DMA((2, 4, 8)),
            pltpu.SemaphoreType.DMA((3, 4)),
            pltpu.SemaphoreType.DMA((7,)),
        ],
        compiler_params=pltpu.CompilerParams(collective_id=0, has_side_effects=True),
        name="gather_all",
    )(tok, cot, wu, wd, ci)


def row_kernel(ci, T, G, wu, wd, H, U, Dn, Tv, Gv, wuv, wdv, xs, gs, ws, hid, gu, gd,
               load, send, recv, loc):
    r, c, xn, yn, dg = place()
    peers = (dg, xn, yn)
    loads = []
    for n, (src, dst) in enumerate(((T, Tv), (wu, wuv), (G, Gv), (wd, wdv))):
        for g in range(4):
            m = src.shape[0] // 4
            part = pl.ds(g * m, m)
            cp = pltpu.make_async_copy(src.at[part], dst.at[part], load.at[n, g])
            cp.start()
            loads.append(cp)
    greet([(p, c) for p in peers])

    def parts(i, p, src):
        row = src * 4 + i
        return (
            (gu.at[i, p], U.at[row]),
            (gd.at[i, p], Dn.at[row]),
            (hid.at[i, p], H.at[:, pl.ds(pl.multiple_of(row * 128, 128), 128)]),
        )

    def puts(i):
        cps = []
        for n, p in enumerate(peers):
            for j, (src, dst) in enumerate(parts(i, p, r)):
                cps.append(pltpu.make_async_remote_copy(
                    src_ref=src, dst_ref=dst, send_sem=send.at[i, n, j], recv_sem=recv.at[i, r, j],
                    device_id=(p, c), device_id_type=MESH))
        for j, (src, dst) in enumerate(parts(i, r, r)):
            cps.append(pltpu.make_async_copy(src, dst, loc.at[i, j]))
        return cps

    def pick(i, a, src, dst):
        for k in range(16):
            b = ci[k // 4, a * 4 + k % 4, r * 4 + i]
            dst[:, k * 128:(k + 1) * 128] = src[b].reshape(512, 128)

    for cp in loads:
        cp.wait()

    @pl.loop(0, 4)
    def _(i):
        pick(i, 0, Tv, xs)
        pre = jnp.dot(xs[...], wuv[:, i].reshape(2048, 128), preferred_element_type=f32)
        pick(i, 1, Gv, gs)
        for k in range(16):
            ws[:, k * 128:(k + 1) * 128] = wdv[k // 4, i, k % 4]
        back = lax.dot_general(gs[...], ws[...], (((1,), (1,)), ((), ())), preferred_element_type=f32)
        sig = jax.nn.sigmoid(pre)
        act = (pre * sig).astype(bf16)
        slope = (back * sig * (1.0 + pre * (1.0 - sig))).astype(bf16)
        hid[i] = act.reshape(4, 128, 128)
        act_t = act.T
        slope_t = slope.T
        for k in range(0, 16, 4):
            cols = slice(k * 128, (k + 4) * 128)
            down = jnp.dot(act_t, gs[:, cols], preferred_element_type=f32)
            up = jnp.dot(slope_t, xs[:, cols], preferred_element_type=f32)
            for j in range(4):
                gd[i, k // 4, j] = down[:, j * 128:(j + 1) * 128].astype(bf16)
                gu[i, k // 4, j] = up[:, j * 128:(j + 1) * 128].T.astype(bf16)
        for cp in puts(i):
            cp.start()

    @pl.loop(0, 4)
    def _(i):
        for n, p in enumerate(peers):
            for j, (src, dst) in enumerate(parts(i, p, p)):
                pltpu.make_async_remote_copy(
                    src_ref=dst, dst_ref=dst, send_sem=send.at[i, n, j], recv_sem=recv.at[i, p, j],
                    device_id=(p, c), device_id_type=MESH).wait_recv()
        cps = puts(i)
        for cp in cps[:9]:
            cp.wait_send()
        for cp in cps[9:]:
            cp.wait()


def rows_all(ci, T, G, wu, wd):
    grad = jax.ShapeDtypeStruct((16, 4, 128, 128), bf16)
    out = pltpu.VMEM((4, 4, 4, 128, 128), bf16)
    return pl.pallas_call(
        row_kernel,
        out_shape=(jax.ShapeDtypeStruct((128, 2048), bf16), grad, grad),
        in_specs=[pl.BlockSpec(memory_space=pltpu.SMEM), ANY, ANY, ANY, ANY],
        out_specs=(ANY,) * 3,
        scratch_shapes=[
            pltpu.VMEM(T.shape, bf16), pltpu.VMEM(G.shape, bf16),
            pltpu.VMEM(wu.shape, bf16), pltpu.VMEM(wd.shape, bf16),
            pltpu.VMEM((512, 2048), bf16), pltpu.VMEM((512, 2048), bf16),
            pltpu.VMEM((128, 2048), bf16),
            pltpu.VMEM((4, 4, 128, 128), bf16), out, out,
            pltpu.SemaphoreType.DMA((4, 4)),
            pltpu.SemaphoreType.DMA((4, 3, 3)),
            pltpu.SemaphoreType.DMA((4, 4, 3)),
            pltpu.SemaphoreType.DMA((4, 3)),
        ],
        compiler_params=pltpu.CompilerParams(
            collective_id=1, has_side_effects=True, vmem_limit_bytes=56 << 20),
        name="rows_all",
    )(ci, T, G, wu, wd)


def blocked(rows):
    return rows.reshape(128, 8, 128).transpose(1, 0, 2)


def per_row(tokens, cotangent, up_blocks, up_cols, down_blocks, down_cols):
    wu = up_blocks.reshape(4, 4, 4, 128, 128)
    wd = down_blocks.reshape(4, 4, 4, 128, 128)
    ci = jnp.concatenate([up_cols.T, down_cols.T], axis=0)
    ci = jnp.pad(ci, ((0, 0), (0, 112)))
    T, G, WU, WD, CI = gather_all(blocked(tokens), blocked(cotangent), wu, wd, ci)
    return rows_all(CI, T, G, WU, WD)


def per_device(tokens, cotangent, up_blocks, up_cols, down_blocks, down_cols):
    rows = tokens.shape[0]
    local_rows = up_blocks.shape[0]
    side = up_blocks.shape[2]
    whole_up, up_index, whole_down, down_index = (
        lax.all_gather(up_blocks, "row", axis=1, tiled=True),
        lax.all_gather(up_cols, "row", axis=1, tiled=True),
        lax.all_gather(down_blocks, "row", axis=1, tiled=True),
        lax.all_gather(down_cols, "row", axis=1, tiled=True),
    )
    piece_in = lax.all_gather(tokens, "col", axis=1, tiled=True)
    piece_back = lax.all_gather(cotangent, "col", axis=1, tiled=True)
    width = piece_in.shape[1] // side
    in_piece = piece_in.reshape(rows, width, side)
    back_piece = piece_back.reshape(rows, width, side)
    idents = jnp.arange(width, dtype=jnp.int32)
    pick_up = (up_index[:, :, None] == idents[None, None, :]).astype(jnp.bfloat16)
    pick_down = (down_index[:, :, None] == idents[None, None, :]).astype(jnp.bfloat16)
    in_sel = jnp.einsum(
        "tcd,ikc->tikd", in_piece, pick_up, preferred_element_type=jnp.float32
    ).astype(jnp.bfloat16)
    back_sel = jnp.einsum(
        "tcd,ikc->tikd", back_piece, pick_down, preferred_element_type=jnp.float32
    ).astype(jnp.bfloat16)
    in_sel, back_sel = (in_sel, back_sel)
    pre = jnp.einsum("tikd,ikdf->tif", in_sel, whole_up, preferred_element_type=jnp.float32)
    back = jnp.einsum("tikd,ikfd->tif", back_sel, whole_down, preferred_element_type=jnp.float32)
    act = jax.nn.silu(pre).astype(jnp.bfloat16)
    part_down = jnp.einsum("tif,tikd->ikfd", act, back_sel, preferred_element_type=jnp.float32)
    sig = jax.nn.sigmoid(pre)
    slope = (back * sig * (1.0 + pre * (1.0 - sig))).astype(jnp.bfloat16)
    part_up = jnp.einsum("tikd,tif->ikdf", in_sel, slope, preferred_element_type=jnp.float32)
    grad_up, grad_down = (
        lax.psum_scatter(
            part_up.astype(jnp.bfloat16).astype(jnp.float32).astype(jnp.bfloat16),
            "row",
            scatter_dimension=1,
            tiled=True,
        ).astype(jnp.float32),
        lax.psum_scatter(
            part_down.astype(jnp.bfloat16).astype(jnp.float32).astype(jnp.bfloat16),
            "row",
            scatter_dimension=1,
            tiled=True,
        ).astype(jnp.float32),
    )
    hidden = act.reshape(rows, local_rows * side)
    return (hidden, grad_up.astype(jnp.bfloat16), grad_down.astype(jnp.bfloat16))


def solution(mesh):
    small = mesh.shape["row"] == 4 and mesh.shape["col"] == 8
    return jax.shard_map(
        per_row if small else per_device,
        mesh=mesh,
        in_specs=(
            P("row", "col"),
            P("row", "col"),
            P("col", "row", None, None),
            P("col", "row"),
            P("col", "row", None, None),
            P("col", "row"),
        ),
        out_specs=(P("row", "col"), P("col", "row", None, None), P("col", "row", None, None)),
        check_vma=False,
    )
```

```python
import functools

import jax
import jax.numpy as jnp
from jax import lax
from jax.experimental import pallas as pl
from jax.experimental.pallas import tpu as pltpu
from jax.sharding import PartitionSpec as P

MESH = pl.DeviceIdType.MESH
ANY = pl.BlockSpec(memory_space=pl.ANY)
f32 = jnp.float32
bf16 = jnp.bfloat16


def place():
    r = lax.axis_index("row")
    c = lax.axis_index("col")
    xn = r + 1 - 2 * (r % 2)
    yn = (r + 2) % 4
    return r, c, xn, yn, 3 - r


class Puts:
    def __init__(self, sems):
        self.sems = sems
        self.copies = []

    def __call__(self, src, dst, recv, dev, when=None):
        cp = pltpu.make_async_remote_copy(
            src_ref=src, dst_ref=dst, send_sem=self.sems.at[len(self.copies)],
            recv_sem=recv, device_id=dev, device_id_type=MESH)
        if when is None:
            cp.start()
        else:
            pl.when(when)(cp.start)
        self.copies.append((cp, when))

    def got(self, ref, recv, dev):
        pltpu.make_async_remote_copy(
            src_ref=ref, dst_ref=ref, send_sem=self.sems.at[0],
            recv_sem=recv, device_id=dev, device_id_type=MESH).wait_recv()

    def drain(self):
        for cp, when in self.copies:
            if when is None:
                cp.wait_send()
            else:
                pl.when(when)(cp.wait_send)


def greet(devs):
    sem = pltpu.get_barrier_semaphore()
    for dev in devs:
        pl.semaphore_signal(sem, inc=1, device_id=dev, device_id_type=MESH)
    pl.semaphore_wait(sem, len(devs))


def layer_kernel(tokens, cotangent, wu, wd, ci, H, U, Dn, tok, cot, T, G, WU, WD, CI, cols,
                 xs, gs, ws, hid, gu, gd, send, recv, wrecv, loc, gsend, grecv, gloc):
    r, c, xn, yn, dg = place()
    z, q = c // 2, c % 2
    pc = c + 1 - 2 * q
    first = xn + q * (yn - xn)
    second = yn + q * (xn - yn)
    zcs = [((z + d) % 4) * 2 + q for d in range(4)]
    X, Y, D, Q = (xn, c), (yn, c), (dg, c), (r, pc)
    rows = (r, xn, yn, dg)
    put = Puts(send)

    def slot(a, rr, cc):
        return (T, G)[a].at[pl.ds(cc * 8, 8), rr]

    def fwd(a, rr, cc, dev, src=None, when=None):
        ref = slot(a, rr, cc)
        put(ref if src is None else src, ref, recv.at[a, rr, cc], dev, when)

    def got(a, rr, cc):
        put.got(slot(a, rr, cc), recv.at[a, rr, cc], Q)

    ins = []
    for a, (src, dst) in enumerate(((cotangent, cot), (tokens, tok))):
        for j in range(8):
            cp = pltpu.make_async_copy(src.at[:, j * 128:(j + 1) * 128], dst.at[j], loc.at[a * 8 + j])
            cp.start()
            ins.append(cp)
    greet([(r, zc) for zc in zcs[1:]] + [X, Y, D, Q])
    for cp in ins:
        cp.wait()
    outs = [
        pltpu.make_async_copy(tok, slot(0, r, c), loc.at[16]),
        pltpu.make_async_copy(cot, slot(1, r, c), loc.at[17]),
        pltpu.make_async_copy(ci, CI.at[r], loc.at[18]),
        pltpu.make_async_copy(wu.at[r], WU.at[r], loc.at[19]),
        pltpu.make_async_copy(wd.at[r], WD.at[r], loc.at[20]),
    ]
    for cp in outs:
        cp.start()

    def along(rr, src=None):
        fwd(1, rr, c, (r, c + 2), src, z < 3)
        fwd(1, rr, c, (r, c - 2), src, z > 0)

    def weights(h):
        half = pl.ds(2 * h, 2)
        for j in range(2):
            for peer in (dg, xn, yn):
                put((wu, wd)[j].at[peer, half], (WU, WD)[j].at[r, half], wrecv.at[2 * h + j, r], (peer, c))

    def weights_in(h):
        half = pl.ds(2 * h, 2)
        for j in range(2):
            for peer in (dg, xn, yn):
                put.got((WU, WD)[j].at[peer, half], wrecv.at[2 * h + j, peer], (peer, c))

    fwd(1, r, c, X, cot)
    fwd(1, r, c, Y, cot)
    for d in (1, 3, 2):
        fwd(0, r, c, (r, zcs[d]), tok)
    fwd(0, r, c, X, tok)
    fwd(0, r, c, Y, tok)
    along(r, cot)
    fwd(0, r, c, Q, tok)
    fwd(1, r, c, Q, cot)
    for peer in (dg, xn, yn):
        put(ci, CI.at[r], wrecv.at[4, r], (peer, c))
    got(1, first, c)
    fwd(1, first, c, (second, c))
    got(1, second, c)
    for rr in (first, second):
        along(rr)
        fwd(1, rr, c, Q)
    weights(0)
    got(1, dg, c)
    along(dg)
    fwd(1, dg, c, Q)
    def relay(d):
        got(0, first, zcs[d])
        fwd(0, first, zcs[d], (second, c))
        fwd(0, first, zcs[d], Q)

    def onward(step):
        for sign in (1, -1):
            here = z >= step if sign == 1 else z + step < 4
            more = z < 3 if sign == 1 else z > 0
            cc = c - 2 * sign * step
            for rr in rows:
                pl.when(here)(functools.partial(got, 1, rr, cc))
                if step < 3:
                    fwd(1, rr, cc, (r, c + 2 * sign), None, here & more)
                fwd(1, rr, cc, Q, None, here)

    for d in (1, 3, 2):
        got(0, r, zcs[d])
        fwd(0, r, zcs[d], X)
        fwd(0, r, zcs[d], Y)
        fwd(0, r, zcs[d], Q)
    relay(0)
    relay(1)
    onward(1)
    relay(3)
    relay(2)
    weights(1)
    for d in (0, 1):
        for rr in (second, dg):
            got(0, rr, zcs[d])
            fwd(0, rr, zcs[d], Q)
    onward(2)
    for d in (3, 2):
        for rr in (second, dg):
            got(0, rr, zcs[d])
            fwd(0, rr, zcs[d], Q)
    onward(3)
    for peer in (dg, xn, yn):
        put.got(CI.at[peer], wrecv.at[4, peer], (peer, c))
    for cp in outs:
        cp.wait()
    table = pltpu.make_async_copy(CI, cols, loc.at[21])
    table.start()
    weights_in(0)
    table.wait()
    for a in range(2):
        for d in range(4):
            for rr in rows:
                got(a, rr, ((z + d) % 4) * 2 + 1 - q)
    peers = (dg, xn, yn)

    def parts(i, p, src):
        row = src * 4 + i
        return (
            (gu.at[i, p], U.at[row]),
            (gd.at[i, p], Dn.at[row]),
            (hid.at[i, p], H.at[:, pl.ds(pl.multiple_of(row * 128, 128), 128)]),
        )

    def puts(i):
        cps = []
        for n, p in enumerate(peers):
            for j, (src, dst) in enumerate(parts(i, p, r)):
                cps.append(pltpu.make_async_remote_copy(
                    src_ref=src, dst_ref=dst, send_sem=gsend.at[i, n, j], recv_sem=grecv.at[i, r, j],
                    device_id=(p, c), device_id_type=MESH))
        for j, (src, dst) in enumerate(parts(i, r, r)):
            cps.append(pltpu.make_async_copy(src, dst, gloc.at[i, j]))
        return cps

    def pick(i, a, src, dst):
        for k in range(16):
            b = cols[k // 4, a * 4 + k % 4, r * 4 + i]
            dst[:, k * 128:(k + 1) * 128] = src[b].reshape(512, 128)

    @pl.loop(0, 4)
    def _(i):
        pl.when(i == 2)(functools.partial(weights_in, 1))
        pick(i, 0, T, xs)
        pre = jnp.dot(xs[...], WU[:, i].reshape(2048, 128), preferred_element_type=f32)
        pick(i, 1, G, gs)
        for k in range(16):
            ws[:, k * 128:(k + 1) * 128] = WD[k // 4, i, k % 4]
        back = lax.dot_general(gs[...], ws[...], (((1,), (1,)), ((), ())), preferred_element_type=f32)
        sig = jax.nn.sigmoid(pre)
        act = (pre * sig).astype(bf16)
        slope = (back * sig * (1.0 + pre * (1.0 - sig))).astype(bf16)
        hid[i] = act.reshape(4, 128, 128)
        act_t = act.T
        slope_t = slope.T
        for k in range(0, 16, 4):
            cols = slice(k * 128, (k + 4) * 128)
            down = jnp.dot(act_t, gs[:, cols], preferred_element_type=f32)
            up = jnp.dot(slope_t, xs[:, cols], preferred_element_type=f32)
            for j in range(4):
                gd[i, k // 4, j] = down[:, j * 128:(j + 1) * 128].astype(bf16)
                gu[i, k // 4, j] = up[:, j * 128:(j + 1) * 128].T.astype(bf16)
        for cp in puts(i):
            cp.start()

    @pl.loop(0, 4)
    def _(i):
        for n, p in enumerate(peers):
            for j, (src, dst) in enumerate(parts(i, p, p)):
                pltpu.make_async_remote_copy(
                    src_ref=dst, dst_ref=dst, send_sem=gsend.at[i, n, j], recv_sem=grecv.at[i, p, j],
                    device_id=(p, c), device_id_type=MESH).wait_recv()
        cps = puts(i)
        for cp in cps[:9]:
            cp.wait_send()
        for cp in cps[9:]:
            cp.wait()


    put.drain()


def layer(tokens, cotangent, wu, wd, ci):
    grad = jax.ShapeDtypeStruct((16, 4, 128, 128), bf16)
    unit = pltpu.VMEM((8, 128, 128), bf16)
    full = pltpu.VMEM((64, 4, 128, 128), bf16)
    weight = pltpu.VMEM(wu.shape, bf16)
    picked = pltpu.VMEM((512, 2048), bf16)
    return pl.pallas_call(
        layer_kernel,
        out_shape=(jax.ShapeDtypeStruct((128, 2048), bf16), grad, grad),
        in_specs=[ANY] * 5,
        out_specs=(ANY,) * 3,
        scratch_shapes=[
            unit, unit, full, full, weight, weight,
            pltpu.VMEM((4, 8, 128), jnp.int32), pltpu.SMEM((4, 8, 128), jnp.int32),
            picked, picked, pltpu.VMEM((128, 2048), bf16),
            pltpu.VMEM((4, 4, 128, 128), bf16), weight, weight,
            pltpu.SemaphoreType.DMA((104,)),
            pltpu.SemaphoreType.DMA((2, 4, 8)),
            pltpu.SemaphoreType.DMA((5, 4)),
            pltpu.SemaphoreType.DMA((22,)),
            pltpu.SemaphoreType.DMA((4, 3, 3)),
            pltpu.SemaphoreType.DMA((4, 4, 3)),
            pltpu.SemaphoreType.DMA((4, 3)),
        ],
        compiler_params=pltpu.CompilerParams(
            collective_id=0, has_side_effects=True, vmem_limit_bytes=56 << 20),
        name="layer",
    )(tokens, cotangent, wu, wd, ci)


def per_row(tokens, cotangent, up_blocks, up_cols, down_blocks, down_cols):
    wu = up_blocks.reshape(4, 4, 4, 128, 128)
    wd = down_blocks.reshape(4, 4, 4, 128, 128)
    ci = jnp.concatenate([up_cols.T, down_cols.T], axis=0)
    ci = jnp.pad(ci, ((0, 0), (0, 112)))
    return layer(tokens, cotangent, wu, wd, ci)


def per_device(tokens, cotangent, up_blocks, up_cols, down_blocks, down_cols):
    rows = tokens.shape[0]
    local_rows = up_blocks.shape[0]
    side = up_blocks.shape[2]
    whole_up, up_index, whole_down, down_index = (
        lax.all_gather(up_blocks, "row", axis=1, tiled=True),
        lax.all_gather(up_cols, "row", axis=1, tiled=True),
        lax.all_gather(down_blocks, "row", axis=1, tiled=True),
        lax.all_gather(down_cols, "row", axis=1, tiled=True),
    )
    piece_in = lax.all_gather(tokens, "col", axis=1, tiled=True)
    piece_back = lax.all_gather(cotangent, "col", axis=1, tiled=True)
    width = piece_in.shape[1] // side
    in_piece = piece_in.reshape(rows, width, side)
    back_piece = piece_back.reshape(rows, width, side)
    idents = jnp.arange(width, dtype=jnp.int32)
    pick_up = (up_index[:, :, None] == idents[None, None, :]).astype(jnp.bfloat16)
    pick_down = (down_index[:, :, None] == idents[None, None, :]).astype(jnp.bfloat16)
    in_sel = jnp.einsum(
        "tcd,ikc->tikd", in_piece, pick_up, preferred_element_type=jnp.float32
    ).astype(jnp.bfloat16)
    back_sel = jnp.einsum(
        "tcd,ikc->tikd", back_piece, pick_down, preferred_element_type=jnp.float32
    ).astype(jnp.bfloat16)
    in_sel, back_sel = (in_sel, back_sel)
    pre = jnp.einsum("tikd,ikdf->tif", in_sel, whole_up, preferred_element_type=jnp.float32)
    back = jnp.einsum("tikd,ikfd->tif", back_sel, whole_down, preferred_element_type=jnp.float32)
    act = jax.nn.silu(pre).astype(jnp.bfloat16)
    part_down = jnp.einsum("tif,tikd->ikfd", act, back_sel, preferred_element_type=jnp.float32)
    sig = jax.nn.sigmoid(pre)
    slope = (back * sig * (1.0 + pre * (1.0 - sig))).astype(jnp.bfloat16)
    part_up = jnp.einsum("tikd,tif->ikdf", in_sel, slope, preferred_element_type=jnp.float32)
    grad_up, grad_down = (
        lax.psum_scatter(
            part_up.astype(jnp.bfloat16).astype(jnp.float32).astype(jnp.bfloat16),
            "row",
            scatter_dimension=1,
            tiled=True,
        ).astype(jnp.float32),
        lax.psum_scatter(
            part_down.astype(jnp.bfloat16).astype(jnp.float32).astype(jnp.bfloat16),
            "row",
            scatter_dimension=1,
            tiled=True,
        ).astype(jnp.float32),
    )
    hidden = act.reshape(rows, local_rows * side)
    return (hidden, grad_up.astype(jnp.bfloat16), grad_down.astype(jnp.bfloat16))


def solution(mesh):
    small = mesh.shape["row"] == 4 and mesh.shape["col"] == 8
    return jax.shard_map(
        per_row if small else per_device,
        mesh=mesh,
        in_specs=(
            P("row", "col"),
            P("row", "col"),
            P("col", "row", None, None),
            P("col", "row"),
            P("col", "row", None, None),
            P("col", "row"),
        ),
        out_specs=(P("row", "col"), P("col", "row", None, None), P("col", "row", None, None)),
        check_vma=False,
    )
```

```python
import functools

import jax
import jax.numpy as jnp
from jax import lax
from jax.experimental import pallas as pl
from jax.experimental.pallas import tpu as pltpu
from jax.sharding import PartitionSpec as P

MESH = pl.DeviceIdType.MESH
ANY = pl.BlockSpec(memory_space=pl.ANY)
f32 = jnp.float32
bf16 = jnp.bfloat16


def place():
    r = lax.axis_index("row")
    c = lax.axis_index("col")
    xn = r + 1 - 2 * (r % 2)
    yn = (r + 2) % 4
    return r, c, xn, yn, 3 - r


class Puts:
    def __init__(self, sems):
        self.sems = sems
        self.copies = []

    def __call__(self, src, dst, recv, dev, when=None):
        cp = pltpu.make_async_remote_copy(
            src_ref=src, dst_ref=dst, send_sem=self.sems.at[len(self.copies)],
            recv_sem=recv, device_id=dev, device_id_type=MESH)
        if when is None:
            cp.start()
        else:
            pl.when(when)(cp.start)
        self.copies.append((cp, when))

    def got(self, ref, recv, dev):
        pltpu.make_async_remote_copy(
            src_ref=ref, dst_ref=ref, send_sem=self.sems.at[0],
            recv_sem=recv, device_id=dev, device_id_type=MESH).wait_recv()

    def drain(self):
        for cp, when in self.copies:
            if when is None:
                cp.wait_send()
            else:
                pl.when(when)(cp.wait_send)


def greet(devs):
    sem = pltpu.get_barrier_semaphore()
    for dev in devs:
        pl.semaphore_signal(sem, inc=1, device_id=dev, device_id_type=MESH)
    pl.semaphore_wait(sem, len(devs))


def layer_kernel(tokens, cotangent, wu, wd, ci, H, U, Dn, tok, cot, T, G, WU, WD, CI, cols,
                 xs, gs, ws, hid, gu, gd, send, recv, wrecv, loc, gsend, grecv, gloc):
    r, c, xn, yn, dg = place()
    z, q = c // 2, c % 2
    pc = c + 1 - 2 * q
    first = xn + q * (yn - xn)
    second = yn + q * (xn - yn)
    zcs = [((z + d) % 4) * 2 + q for d in range(4)]
    X, Y, D, Q = (xn, c), (yn, c), (dg, c), (r, pc)
    rows = (r, xn, yn, dg)
    put = Puts(send)

    def slot(a, rr, cc):
        return (T, G)[a].at[pl.ds(cc * 8, 8), rr]

    def fwd(a, rr, cc, dev, src=None, when=None):
        ref = slot(a, rr, cc)
        put(ref if src is None else src, ref, recv.at[a, rr, cc], dev, when)

    def got(a, rr, cc):
        put.got(slot(a, rr, cc), recv.at[a, rr, cc], Q)

    ins = []
    for a, (src, dst) in enumerate(((cotangent, cot), (tokens, tok))):
        for j in range(8):
            cp = pltpu.make_async_copy(src.at[:, j * 128:(j + 1) * 128], dst.at[j], loc.at[a * 8 + j])
            cp.start()
            ins.append(cp)
    greet([(r, zc) for zc in zcs[1:]] + [X, Y, D, Q])
    for cp in ins:
        cp.wait()
    outs = [
        pltpu.make_async_copy(tok, slot(0, r, c), loc.at[16]),
        pltpu.make_async_copy(cot, slot(1, r, c), loc.at[17]),
        pltpu.make_async_copy(ci, CI.at[r], loc.at[18]),
        pltpu.make_async_copy(wu.at[r], WU.at[r], loc.at[19]),
        pltpu.make_async_copy(wd.at[r], WD.at[r], loc.at[20]),
    ]
    for cp in outs:
        cp.start()

    def along(rr, src=None):
        fwd(1, rr, c, (r, c + 2), src, z < 3)
        fwd(1, rr, c, (r, c - 2), src, z > 0)

    def weights(h):
        half = pl.ds(2 * h, 2)
        for j in range(2):
            for peer in (dg, xn, yn):
                put((wu, wd)[j].at[peer, half], (WU, WD)[j].at[r, half], wrecv.at[2 * h + j, r], (peer, c))

    def weights_in(h):
        half = pl.ds(2 * h, 2)
        for j in range(2):
            for peer in (dg, xn, yn):
                put.got((WU, WD)[j].at[peer, half], wrecv.at[2 * h + j, peer], (peer, c))

    fwd(1, r, c, X, cot)
    fwd(1, r, c, Y, cot)
    for d in (1, 3, 2):
        fwd(0, r, c, (r, zcs[d]), tok)
    fwd(0, r, c, X, tok)
    fwd(0, r, c, Y, tok)
    along(r, cot)
    fwd(0, r, c, Q, tok)
    fwd(1, r, c, Q, cot)
    for peer in (dg, xn, yn):
        put(ci, CI.at[r], wrecv.at[4, r], (peer, c))
    got(1, first, c)
    fwd(1, first, c, (second, c))
    got(1, second, c)
    for rr in (first, second):
        along(rr)
        fwd(1, rr, c, Q)
    weights(0)
    got(1, dg, c)
    along(dg)
    fwd(1, dg, c, Q)
    def relay(d):
        got(0, first, zcs[d])
        fwd(0, first, zcs[d], (second, c))
        fwd(0, first, zcs[d], Q)

    def onward(step):
        for sign in (1, -1):
            here = z >= step if sign == 1 else z + step < 4
            more = z < 3 if sign == 1 else z > 0
            cc = c - 2 * sign * step
            for rr in rows:
                pl.when(here)(functools.partial(got, 1, rr, cc))
                if step < 3:
                    fwd(1, rr, cc, (r, c + 2 * sign), None, here & more)
                fwd(1, rr, cc, Q, None, here)

    for d in (1, 3, 2):
        got(0, r, zcs[d])
        fwd(0, r, zcs[d], X)
        fwd(0, r, zcs[d], Y)
        fwd(0, r, zcs[d], Q)
    relay(0)
    relay(1)
    onward(1)
    relay(3)
    relay(2)
    weights(1)
    for d in (0, 1):
        for rr in (second, dg):
            got(0, rr, zcs[d])
            fwd(0, rr, zcs[d], Q)
    onward(2)
    for d in (3, 2):
        for rr in (second, dg):
            got(0, rr, zcs[d])
            fwd(0, rr, zcs[d], Q)
    onward(3)
    for peer in (dg, xn, yn):
        put.got(CI.at[peer], wrecv.at[4, peer], (peer, c))
    for cp in outs:
        cp.wait()
    table = pltpu.make_async_copy(CI, cols, loc.at[21])
    table.start()
    weights_in(0)
    table.wait()
    for a in range(2):
        for d in range(4):
            for rr in rows:
                got(a, rr, ((z + d) % 4) * 2 + 1 - q)
    peers = (dg, xn, yn)

    def parts(i, p, src):
        row = src * 4 + i
        return (
            (gu.at[i, p], U.at[row]),
            (gd.at[i, p], Dn.at[row]),
            (hid.at[i, p], H.at[:, pl.ds(pl.multiple_of(row * 128, 128), 128)]),
        )

    def puts(i):
        cps = []
        for n, p in enumerate(peers):
            for j, (src, dst) in enumerate(parts(i, p, r)):
                cps.append(pltpu.make_async_remote_copy(
                    src_ref=src, dst_ref=dst, send_sem=gsend.at[i, n, j], recv_sem=grecv.at[i, r, j],
                    device_id=(p, c), device_id_type=MESH))
        for j, (src, dst) in enumerate(parts(i, r, r)):
            cps.append(pltpu.make_async_copy(src, dst, gloc.at[i, j]))
        return cps

    def pick(i, a, src, dst):
        for k in range(16):
            b = cols[k // 4, a * 4 + k % 4, r * 4 + i]
            dst[:, k * 128:(k + 1) * 128] = src[b].reshape(512, 128)

    @pl.loop(0, 4)
    def _(i):
        pl.when(i == 2)(functools.partial(weights_in, 1))
        pick(i, 0, T, xs)
        pre = jnp.dot(xs[...], WU[:, i].reshape(2048, 128), preferred_element_type=f32)
        pick(i, 1, G, gs)
        for k in range(16):
            ws[:, k * 128:(k + 1) * 128] = WD[k // 4, i, k % 4]
        back = lax.dot_general(gs[...], ws[...], (((1,), (1,)), ((), ())), preferred_element_type=f32)
        sig = jax.nn.sigmoid(pre)
        act = (pre * sig).astype(bf16)
        slope = (back * sig * (1.0 + pre * (1.0 - sig))).astype(bf16)
        hid[i] = act.reshape(4, 128, 128)
        act_t = act.T
        slope_t = slope.T
        for k in range(0, 16, 4):
            cols = slice(k * 128, (k + 4) * 128)
            down = jnp.dot(act_t, gs[:, cols], preferred_element_type=f32)
            up = jnp.dot(slope_t, xs[:, cols], preferred_element_type=f32)
            for j in range(4):
                gd[i, k // 4, j] = down[:, j * 128:(j + 1) * 128].astype(bf16)
                gu[i, k // 4, j] = up[:, j * 128:(j + 1) * 128].T.astype(bf16)
        for cp in puts(i):
            cp.start()

    @pl.loop(0, 4)
    def _(i):
        for n, p in enumerate(peers):
            for j, (src, dst) in enumerate(parts(i, p, p)):
                pltpu.make_async_remote_copy(
                    src_ref=dst, dst_ref=dst, send_sem=gsend.at[i, n, j], recv_sem=grecv.at[i, p, j],
                    device_id=(p, c), device_id_type=MESH).wait_recv()
        cps = puts(i)
        for cp in cps[:9]:
            cp.wait_send()
        for cp in cps[9:]:
            cp.wait()


    put.drain()


def layer(tokens, cotangent, wu, wd, ci):
    grad = jax.ShapeDtypeStruct((16, 4, 128, 128), bf16)
    unit = pltpu.VMEM((8, 128, 128), bf16)
    full = pltpu.VMEM((64, 4, 128, 128), bf16)
    weight = pltpu.VMEM(wu.shape, bf16)
    picked = pltpu.VMEM((512, 2048), bf16)
    return pl.pallas_call(
        layer_kernel,
        out_shape=(jax.ShapeDtypeStruct((128, 2048), bf16), grad, grad),
        in_specs=[ANY] * 5,
        out_specs=(ANY,) * 3,
        scratch_shapes=[
            unit, unit, full, full, weight, weight,
            pltpu.VMEM((4, 8, 128), jnp.int32), pltpu.SMEM((4, 8, 128), jnp.int32),
            picked, picked, pltpu.VMEM((128, 2048), bf16),
            pltpu.VMEM((4, 4, 128, 128), bf16), weight, weight,
            pltpu.SemaphoreType.DMA((104,)),
            pltpu.SemaphoreType.DMA((2, 4, 8)),
            pltpu.SemaphoreType.DMA((5, 4)),
            pltpu.SemaphoreType.DMA((22,)),
            pltpu.SemaphoreType.DMA((4, 3, 3)),
            pltpu.SemaphoreType.DMA((4, 4, 3)),
            pltpu.SemaphoreType.DMA((4, 3)),
        ],
        compiler_params=pltpu.CompilerParams(
            collective_id=0, has_side_effects=True, vmem_limit_bytes=56 << 20),
        name="layer",
    )(tokens, cotangent, wu, wd, ci)


def settle_kernel(h, u, d, H, U, Dn, vh, vu, vd, si, so):
    pieces = []
    for n, (src, via, dst) in enumerate(((u, vu, U), (d, vd, Dn), (h, vh, H))):
        m = src.shape[0] // 4
        for g in range(4):
            part = pl.ds(g * m, m)
            a = pltpu.make_async_copy(src.at[part], via.at[part], si.at[n, g])
            a.start()
            pieces.append((a, pltpu.make_async_copy(via.at[part], dst.at[part], so.at[n, g])))
    for a, z in pieces:
        a.wait()
        z.start()
    for _, z in pieces:
        z.wait()


def settle(*outs):
    return pl.pallas_call(
        settle_kernel,
        out_shape=tuple(jax.ShapeDtypeStruct(o.shape, o.dtype) for o in outs),
        in_specs=[ANY] * 3,
        out_specs=(ANY,) * 3,
        scratch_shapes=[pltpu.VMEM(o.shape, o.dtype) for o in outs]
        + [pltpu.SemaphoreType.DMA((3, 4))] * 2,
        compiler_params=pltpu.CompilerParams(vmem_limit_bytes=56 << 20),
        name="settle",
    )(*outs)


def per_row(tokens, cotangent, up_blocks, up_cols, down_blocks, down_cols):
    wu = up_blocks.reshape(4, 4, 4, 128, 128)
    wd = down_blocks.reshape(4, 4, 4, 128, 128)
    ci = jnp.concatenate([up_cols.T, down_cols.T], axis=0)
    ci = jnp.pad(ci, ((0, 0), (0, 112)))
    return settle(*layer(tokens, cotangent, wu, wd, ci))


def per_device(tokens, cotangent, up_blocks, up_cols, down_blocks, down_cols):
    rows = tokens.shape[0]
    local_rows = up_blocks.shape[0]
    side = up_blocks.shape[2]
    whole_up, up_index, whole_down, down_index = (
        lax.all_gather(up_blocks, "row", axis=1, tiled=True),
        lax.all_gather(up_cols, "row", axis=1, tiled=True),
        lax.all_gather(down_blocks, "row", axis=1, tiled=True),
        lax.all_gather(down_cols, "row", axis=1, tiled=True),
    )
    piece_in = lax.all_gather(tokens, "col", axis=1, tiled=True)
    piece_back = lax.all_gather(cotangent, "col", axis=1, tiled=True)
    width = piece_in.shape[1] // side
    in_piece = piece_in.reshape(rows, width, side)
    back_piece = piece_back.reshape(rows, width, side)
    idents = jnp.arange(width, dtype=jnp.int32)
    pick_up = (up_index[:, :, None] == idents[None, None, :]).astype(jnp.bfloat16)
    pick_down = (down_index[:, :, None] == idents[None, None, :]).astype(jnp.bfloat16)
    in_sel = jnp.einsum(
        "tcd,ikc->tikd", in_piece, pick_up, preferred_element_type=jnp.float32
    ).astype(jnp.bfloat16)
    back_sel = jnp.einsum(
        "tcd,ikc->tikd", back_piece, pick_down, preferred_element_type=jnp.float32
    ).astype(jnp.bfloat16)
    in_sel, back_sel = (in_sel, back_sel)
    pre = jnp.einsum("tikd,ikdf->tif", in_sel, whole_up, preferred_element_type=jnp.float32)
    back = jnp.einsum("tikd,ikfd->tif", back_sel, whole_down, preferred_element_type=jnp.float32)
    act = jax.nn.silu(pre).astype(jnp.bfloat16)
    part_down = jnp.einsum("tif,tikd->ikfd", act, back_sel, preferred_element_type=jnp.float32)
    sig = jax.nn.sigmoid(pre)
    slope = (back * sig * (1.0 + pre * (1.0 - sig))).astype(jnp.bfloat16)
    part_up = jnp.einsum("tikd,tif->ikdf", in_sel, slope, preferred_element_type=jnp.float32)
    grad_up, grad_down = (
        lax.psum_scatter(
            part_up.astype(jnp.bfloat16).astype(jnp.float32).astype(jnp.bfloat16),
            "row",
            scatter_dimension=1,
            tiled=True,
        ).astype(jnp.float32),
        lax.psum_scatter(
            part_down.astype(jnp.bfloat16).astype(jnp.float32).astype(jnp.bfloat16),
            "row",
            scatter_dimension=1,
            tiled=True,
        ).astype(jnp.float32),
    )
    hidden = act.reshape(rows, local_rows * side)
    return (hidden, grad_up.astype(jnp.bfloat16), grad_down.astype(jnp.bfloat16))


def solution(mesh):
    small = mesh.shape["row"] == 4 and mesh.shape["col"] == 8
    return jax.shard_map(
        per_row if small else per_device,
        mesh=mesh,
        in_specs=(
            P("row", "col"),
            P("row", "col"),
            P("col", "row", None, None),
            P("col", "row"),
            P("col", "row", None, None),
            P("col", "row"),
        ),
        out_specs=(P("row", "col"), P("col", "row", None, None), P("col", "row", None, None)),
        check_vma=False,
    )
```
